32 devices in a mesh: section: 16 (over z, x, core), tensor: 2 (over y).
Axes of the slice: x: 2, y: 2, z: 4, core: 2. Of those that a mesh axis runs over, the one named last changes fastest.
Arguments:
- saved_inputs: bfloat16 [16, 8, 256, 512], P('section', None, 'tensor'), may hold values from -6 to 6
- microbatch_slot: int32 [16, 3], P('section'), may hold values from 0 to 7
- staleness: int32 [16, 2], P('section'), may hold values from 1 to 2
- up_weight: bfloat16 [16, 512, 32768], P('section', None, 'tensor'), may hold values from -0.25 to 0.25
- down_weight: bfloat16 [16, 32768, 512], P('section', 'tensor'), may hold values from -0.03125 to 0.03125
- upstream_grad: bfloat16 [16, 256, 512], P('section', 'tensor'), may hold values from -6 to 6
- head_grad: bfloat16 [2, 256, 512], P(None, 'tensor'), may hold values from -6 to 6
Outputs:
- back_grad: bfloat16 [3, 16, 256, 512], P(None, 'section', 'tensor')
The draws below stay inside these ranges and needn't reach their ends.
All inputs are finite; a program needn't handle non-finite values.
Results may differ from the reference program's by a relative error of at most 0.025.
The reference program's roundings to bfloat16 on the way count: a program that leaves them out, or rounds other values in their place, can miss the bound.
Values may be sent and summed in bfloat16 or wider, within the bound.
A program may use at most 192 MiB of HBM per device.

```python
import math
import jax
import jax.numpy as jnp
from jax import lax

D = 512
FF = 32768
ROWS = 256
SLOTS = 8
TICKS = 3
SECTIONS = 16


def touch_ends(drawn, own_key, smallest, high):
    index_at = [jax.random.randint(jax.random.fold_in(own_key, axis), (), 0, length) for axis, length in enumerate(drawn.shape)]
    main_axis = drawn.shape.index(max(drawn.shape))
    beside = index_at[:main_axis] + [(index_at[main_axis] + 1) % drawn.shape[main_axis]] + index_at[main_axis + 1:]
    return drawn.at[tuple(index_at)].set(smallest).at[tuple(beside)].set(high)


def level_of(own_key, extent, cuts, low, high):
    def one(axis_at, shards_of):
        steps = jax.random.uniform(jax.random.fold_in(jax.random.fold_in(own_key, 6), axis_at), (shards_of,), jnp.float32, low / len(cuts), high / len(cuts))
        return jnp.repeat(jnp.exp(steps), extent[axis_at] // shards_of).reshape((-1,) + (1,) * (len(extent) - axis_at - 1))

    gain = one(*cuts[0])
    for cut in cuts[1:]:
        gain = gain * one(*cut)
    return gain


def centred(rng, shape, scale, limit, cuts=(), dtype=jnp.bfloat16):
    level = level_of(rng, shape, cuts, -0.22, 0.18) if cuts else 1.0
    result = jax.random.normal(rng, shape, jnp.float32) * scale * level
    return jnp.minimum(jnp.maximum(result, -limit), limit).astype(dtype)


def setup_inputs(seed: int = 0) -> dict:
    key_of = jax.random.split(jax.random.key(seed), 8)
    saved_inputs = centred(key_of[0], (SECTIONS, SLOTS, ROWS, D), 1.0, 6.0, ((0, 16), (2, 2)))
    microbatch_slot = touch_ends(jax.random.randint(key_of[1], (SECTIONS, TICKS), 0, SLOTS), jax.random.fold_in(key_of[1], 1), 0, SLOTS - 1).astype(jnp.int32)
    staleness = touch_ends(jax.random.randint(key_of[2], (SECTIONS, TICKS - 1), 1, 3), jax.random.fold_in(key_of[2], 1), 1, 2).astype(jnp.int32)
    up_weight = centred(key_of[3], (SECTIONS, D, FF), D ** -0.5, 0.25, ((0, 16), (2, 2)))
    down_weight = centred(key_of[4], (SECTIONS, FF, D), FF ** -0.5, 0.03125, ((0, 16), (1, 2)))
    upstream_grad = centred(key_of[5], (SECTIONS, ROWS, D), 1.0, 6.0, ((0, 16), (1, 2)))
    head_grad = centred(key_of[6], (TICKS - 1, ROWS, D), 1.0, 6.0, ((1, 2),))
    return dict(saved_inputs=saved_inputs, microbatch_slot=microbatch_slot, staleness=staleness, up_weight=up_weight, down_weight=down_weight, upstream_grad=upstream_grad, head_grad=head_grad)


def learning_rates(total_rows, width, hidden_units):
    up_rate = 0.5 * math.sqrt(hidden_units) / (math.sqrt(total_rows) * width)
    down_rate = 0.5 / (math.sqrt(total_rows) * math.sqrt(hidden_units))
    return (up_rate, down_rate)

def weights_at(tick_index, weight_up, weight_down, gradients, delay_row, rates):
    if tick_index == 0:
        return (weight_up, weight_down)
    total_up = None
    total_down = None
    for earlier in range(tick_index):
        flag = (earlier + delay_row[earlier] <= tick_index).astype(jnp.float32)
        term_up = flag * gradients[earlier][0]
        term_down = flag * gradients[earlier][1]
        total_up = term_up if total_up is None else total_up + term_up
        total_down = term_down if total_down is None else total_down + term_down
    new_up = (weight_up.astype(jnp.float32) - rates[0] * total_up).astype(jnp.bfloat16)
    new_down = (weight_down.astype(jnp.float32) - rates[1] * total_down).astype(jnp.bfloat16)
    return (new_up, new_down)

def section_ticks(incoming, per_section):
    saved, chosen_slots, delay_row, weight_up, weight_down, first_grad = per_section
    rates = learning_rates(saved.shape[1], weight_up.shape[0], weight_up.shape[1])
    grad_out = first_grad
    gradients = []
    outputs = []
    for tick_index in range(TICKS):
        cur_up, cur_down = weights_at(tick_index, weight_up, weight_down, gradients, delay_row, rates)
        inputs = lax.dynamic_index_in_dim(saved, chosen_slots[tick_index], 0, keepdims=False)
        before_relu = jnp.dot(inputs, cur_up, preferred_element_type=jnp.float32)
        hidden_raw = lax.dot_general(grad_out, cur_down, (((1,), (1,)), ((), ())), preferred_element_type=jnp.float32)
        masked = jnp.where(before_relu > 0, hidden_raw, 0.0).astype(jnp.bfloat16)
        back = lax.dot_general(masked, cur_up, (((1,), (1,)), ((), ())), preferred_element_type=jnp.float32)
        outputs.append(back.astype(jnp.bfloat16))
        if tick_index + 1 < TICKS:
            hidden = jnp.maximum(before_relu, 0.0).astype(jnp.bfloat16)
            grad_up = lax.dot_general(inputs, masked, (((0,), (0,)), ((), ())), preferred_element_type=jnp.float32)
            grad_down = lax.dot_general(hidden, grad_out, (((0,), (0,)), ((), ())), preferred_element_type=jnp.float32)
            gradients.append((grad_up, grad_down))
            grad_out = incoming[tick_index]
    stacked = jnp.stack(outputs)
    return (stacked[:TICKS - 1], stacked)

def reference(saved_inputs, microbatch_slot, staleness, up_weight, down_weight, upstream_grad, head_grad):
    _, every = lax.scan(section_ticks, head_grad, (saved_inputs, microbatch_slot, staleness, up_weight, down_weight, upstream_grad), reverse=True)
    return jnp.transpose(every, (1, 0, 2, 3))
```

```python
import functools
import math

import jax
import jax.numpy as jnp
from jax import lax
from jax.experimental import pallas as pl
from jax.experimental.pallas import tpu as pltpu
from jax.sharding import PartitionSpec as P

MESH = pl.DeviceIdType.MESH
F32 = jnp.float32
BF16 = jnp.bfloat16
NT = (((1,), (1,)), ((), ()))


def learning_rates(total_rows, width, hidden_units):
    up_rate = 0.5 * math.sqrt(hidden_units) / (math.sqrt(total_rows) * width)
    down_rate = 0.5 / (math.sqrt(total_rows) * math.sqrt(hidden_units))
    return (up_rate, down_rate)


def dot(a, b):
    return jnp.dot(a, b, preferred_element_type=F32)


def dot_nt(a, b):
    return lax.dot_general(a, b, NT, preferred_element_type=F32)


def kernel(
    sections, parts, ticks, tile, group, rates,
    slot_ref, stale_ref, saved_ref, up_hbm, down_hbm, first_ref, head_ref,
    out_ref, kept_hid, kept_hgr,
    up, down, hid, hgr, x_all, og, xs, ogs, acc, partial, landed, short, short_landed,
    old_hid, old_hgr,
    weight_sem, keep_sem, load_sem,
    x_send, x_recv, og_recv, first_send, head_send, sum_send, sum_recv, back_send,
):
    sec = lax.axis_index("section")
    me = lax.axis_index("tensor")
    is_last = sec == sections - 1
    not_first = sec > 0
    width, hidden = up.shape
    block = first_ref.shape[1]
    rows = block * parts
    chunks = hidden // tile
    wide = group * tile
    steps = hidden // wide
    mid = (3 * steps) // 8

    def at(i, size=tile):
        if isinstance(i, int):
            return pl.ds(i * size, size)
        return pl.ds(pl.multiple_of(i * size, size), size)

    def peer(k):
        return lax.rem(me + k, parts)

    def weight_copies(i):
        return (
            pltpu.make_async_copy(up_hbm.at[0, :, at(i)], up.at[:, at(i)], weight_sem.at[0, i]),
            pltpu.make_async_copy(down_hbm.at[0, at(i), :], down.at[at(i), :], weight_sem.at[1, i]),
        )

    slots = old_hid.shape[0]

    def keep_copies(i):
        return (
            pltpu.make_async_copy(hid.at[at(i, wide), :], kept_hid.at[at(i, wide), :], keep_sem.at[0, i]),
            pltpu.make_async_copy(hgr.at[at(i, wide), :], kept_hgr.at[at(i, wide), :], keep_sem.at[1, i]),
        )

    def load_copies(i):
        s = i % slots
        return (
            pltpu.make_async_copy(kept_hid.at[at(i, wide), :], old_hid.at[s], load_sem.at[0, s]),
            pltpu.make_async_copy(kept_hgr.at[at(i, wide), :], old_hgr.at[s], load_sem.at[1, s]),
        )

    def remote(src, dst, send, recv, s, p):
        return pltpu.make_async_remote_copy(
            src_ref=src, dst_ref=dst, send_sem=send, recv_sem=recv,
            device_id={"section": s, "tensor": p}, device_id_type=MESH,
        )

    def x_copies(t):
        return [
            remote(
                x_all.at[t, me], x_all.at[t, me],
                x_send.at[t, k - 1], x_recv.at[t, me], sec, peer(k),
            )
            for k in range(1, parts)
        ]

    def first_copies():
        return [
            remote(
                first_ref.at[0], og.at[0, me],
                first_send.at[k - 1], og_recv.at[0, me], sec, peer(k),
            )
            for k in range(1, parts)
        ]

    def head_copies(t):
        return [
            remote(
                head_ref.at[t], og.at[t + 1, me],
                head_send.at[t, k - 1], og_recv.at[t + 1, me], sec, peer(k),
            )
            for k in range(1, parts)
        ]

    def sum_copies(t):
        return [
            remote(
                partial.at[peer(k)] if t < ticks - 1 else short.at[peer(k)],
                landed.at[t, k - 1] if t < ticks - 1 else short_landed.at[k - 1],
                sum_send.at[t, k - 1], sum_recv.at[t, k - 1], sec, peer(k),
            )
            for k in range(1, parts)
        ]

    def back_copies(t):
        return [
            remote(
                out_ref.at[t, 0], og.at[t + 1, me],
                back_send.at[t, k], og_recv.at[t + 1, me], sec - 1, peer(k),
            )
            for k in range(parts)
        ]

    def arrived(ref, recv, t, first):
        for k in range(first, parts):
            here = ref.at[t, peer(k)]
            remote(here, here, recv.at[t, peer(k)], recv.at[t, peer(k)], sec, peer(1)).wait_recv()

    def start_weights(i, carry):
        for c in weight_copies(i):
            c.start()
        return carry

    lax.fori_loop(0, chunks, start_weights, 0)
    for t in range(ticks):
        x_all[t, me] = saved_ref[0, slot_ref[0, t]]
    og[0, me] = first_ref[0]

    @pl.when(is_last)
    def _():
        for t in range(ticks - 1):
            og[t + 1, me] = head_ref[t]

    barrier = pltpu.get_barrier_semaphore()
    before = lax.rem(sec + sections - 1, sections)
    after = lax.rem(sec + 1, sections)
    for k in range(1, parts):
        pl.semaphore_signal(
            barrier, inc=1, device_id={"section": sec, "tensor": peer(k)}, device_id_type=MESH
        )
    for other in (before, after):
        for k in range(parts):
            pl.semaphore_signal(
                barrier, inc=1, device_id={"section": other, "tensor": peer(k)},
                device_id_type=MESH,
            )
    pl.semaphore_wait(barrier, 3 * parts - 1)

    for c in x_copies(0) + first_copies():
        c.start()
    for t in range(1, ticks):
        for c in x_copies(t):
            c.start()

    @pl.when(is_last)
    def _():
        for t in range(ticks - 1):
            for c in head_copies(t):
                c.start()

    arrived(x_all, x_recv, 0, 1)

    def x_of(t):
        return x_all[t].reshape(rows, width)

    def og_of(t):
        return og[t].reshape(rows, width)

    def flag(j, t):
        return jnp.where(j + stale_ref[0, j] <= t, 1.0, 0.0).astype(F32)

    def hidden_of(t, i):
        return jnp.maximum(dot(x_of(t), up[:, at(i, wide)]), 0.0).astype(BF16).T

    def grad_of(t, i, h):
        raw = dot_nt(down[at(i, wide), :], og_of(t))
        return jnp.where(h.astype(F32) > 0, raw, 0.0).astype(BF16)

    def add_back(i):
        acc[...] += dot(up[:, at(i, wide)], hgr[at(i, wide), :])

    def run(stage, depth, count=steps):
        for i in range(depth):
            stage(i, range(0, i + 1))

        def inner(i, carry):
            stage(i, range(0, depth + 1))
            return carry

        lax.fori_loop(depth, count, inner, 0)
        for i in range(count, count + depth):
            stage(i, range(i - count + 1, depth + 1))

    def start_sum(t):
        total = acc[...].T.reshape(parts, block, width)
        partial[...] = total
        if t == ticks - 1:
            short[...] = total.astype(BF16)
        for c in sum_copies(t):
            c.start()

    def finish_sum(t):
        for c in sum_copies(t):
            c.wait_recv()
        total = partial[me]
        for k in range(1, parts):
            if t < ticks - 1:
                total = total + landed[t, k - 1]
            else:
                total = total + short_landed[k - 1].astype(F32)
        out_ref[t, 0] = total.astype(BF16)

    def between(t, i):
        @pl.when(i == mid)
        def _():
            finish_sum(t)

            @pl.when(not_first)
            def _():
                for c in back_copies(t):
                    c.start()

    acc[...] = jnp.zeros_like(acc)

    def tick_zero(i, due):
        if 0 in due:
            for k in range(group):
                for c in weight_copies(i * group + k):
                    c.wait()
        if isinstance(i, int) and i == 0:
            arrived(og, og_recv, 0, 1)
        if 1 in due:
            for c in keep_copies(i - 1):
                c.start()
            add_back(i - 1)
        if 0 in due:
            h = hidden_of(0, i)
            hid[at(i, wide), :] = h
            hgr[at(i, wide), :] = grad_of(0, i, h)

    run(tick_zero, 1, steps)
    start_sum(0)
    for t in range(1, ticks):
        arrived(x_all, x_recv, t, 1)

    def turned(t):
        return x_of(t).astype(F32).T.astype(BF16)

    for t in range(1, ticks):
        last = t == ticks - 1
        if last:
            up_step, down_step = rates
            early, late = flag(t - 2, t).astype(BF16), flag(t - 1, t).astype(BF16)
            xs[:, :rows] = xs[:, :rows] * early
            xs[:, rows:] = turned(t - 1) * late
            ogs[:rows, :] = og_of(t - 2) * early
            ogs[rows:, :] = og_of(t - 1) * late
        else:
            xs[:, :rows] = turned(t - 1)
            up_step, down_step = rates[0] * flag(t - 1, t), rates[1] * flag(t - 1, t)

        def renew(i, due, t=t, last=last, up_step=up_step, down_step=down_step):
            if not isinstance(i, int):
                between(t - 1, i)
            if last:
                for c in load_copies(i):
                    c.wait()
                for k in range(group):
                    for c in weight_copies(i * group + k):
                        c.wait()
                s = i % slots
                g = jnp.concatenate([old_hgr[s], hgr[at(i, wide), :]], axis=1)
                h = jnp.concatenate([old_hid[s], hid[at(i, wide), :]], axis=1)
                x_side, og_side = xs[...], ogs[...]
            else:
                for c in keep_copies(i):
                    c.wait()
                g, h = hgr[at(i, wide), :], hid[at(i, wide), :]
                x_side, og_side = xs[:, :rows], og_of(t - 1)
            down[at(i, wide), :] = (
                down[at(i, wide), :].astype(F32) - down_step * dot(h, og_side)
            ).astype(BF16)
            up[:, at(i, wide)] = (
                up[:, at(i, wide)].astype(F32) - up_step * dot_nt(x_side, g)
            ).astype(BF16)
            hid[at(i, wide), :] = hidden_of(t, i)
            if last:
                @pl.when(i + slots < steps)
                def _():
                    for c in load_copies(i + slots):
                        c.start()

        run(renew, 0)

        @pl.when(is_last)
        def _():
            arrived(og, og_recv, t, 1)

        @pl.when(jnp.logical_not(is_last))
        def _():
            arrived(og, og_recv, t, 0)

        acc[...] = jnp.zeros_like(acc)
        for c in sum_copies(t - 1):
            c.wait_send()

        if not last:
            for k in range(min(slots, steps)):
                for c in load_copies(k):
                    c.start()

        def reload(i):
            for k in range(group):
                for c in weight_copies(i * group + k):
                    c.start()

        def tick(i, due, t=t, last=last):
            if not last:
                if isinstance(i, int):
                    if i >= 2:
                        reload(i - 2)
                else:
                    @pl.when(i >= 2)
                    def _():
                        reload(i - 2)
            if 1 in due:
                add_back(i - 1)
            if 0 in due:
                hgr[at(i, wide), :] = grad_of(t, i, hid[at(i, wide), :])

        run(tick, 1, steps)
        if not last:
            reload(steps - 1)
        start_sum(t)

    finish_sum(ticks - 1)

    for t in range(ticks):
        for c in x_copies(t):
            c.wait_send()
    for c in sum_copies(ticks - 1):
        c.wait_send()
    for c in first_copies():
        c.wait_send()
    for t in range(ticks - 1):
        @pl.when(is_last)
        def _():
            for c in head_copies(t):
                c.wait_send()

        @pl.when(not_first)
        def _():
            for c in back_copies(t):
                c.wait_send()


def body(
    saved_inputs, microbatch_slot, staleness, up_weight, down_weight, upstream_grad, head_grad
):
    block = saved_inputs.shape[2]
    ticks = microbatch_slot.shape[1]
    sections = lax.axis_size("section")
    parts = lax.axis_size("tensor")
    width, hidden = up_weight.shape[1:]
    rows = block * parts
    tile = min(512, hidden)
    group = min(4, hidden // tile)
    wide = group * tile
    chunks = hidden // tile
    steps = hidden // wide
    slots = 2
    rates = learning_rates(rows, width, hidden * parts)
    vmem = pl.BlockSpec(memory_space=pltpu.VMEM)
    smem = pl.BlockSpec(memory_space=pltpu.SMEM)
    hbm = pl.BlockSpec(memory_space=pl.ANY)
    dma = pltpu.SemaphoreType.DMA
    out, _, _ = pl.pallas_call(
        functools.partial(kernel, sections, parts, ticks, tile, group, rates),
        out_shape=(
            jax.ShapeDtypeStruct((ticks, 1, block, width), BF16),
            jax.ShapeDtypeStruct((hidden, rows), BF16),
            jax.ShapeDtypeStruct((hidden, rows), BF16),
        ),
        in_specs=[smem, smem, vmem, hbm, hbm, vmem, vmem],
        out_specs=(vmem, hbm, hbm),
        scratch_shapes=[
            pltpu.VMEM((width, hidden), BF16),
            pltpu.VMEM((hidden, width), BF16),
            pltpu.VMEM((hidden, rows), BF16),
            pltpu.VMEM((hidden, rows), BF16),
            pltpu.VMEM((ticks, parts, block, width), BF16),
            pltpu.VMEM((ticks, parts, block, width), BF16),
            pltpu.VMEM((width, 2 * rows), BF16),
            pltpu.VMEM((2 * rows, width), BF16),
            pltpu.VMEM((width, rows), F32),
            pltpu.VMEM((parts, block, width), F32),
            pltpu.VMEM((ticks - 1, max(parts - 1, 1), block, width), F32),
            pltpu.VMEM((parts, block, width), BF16),
            pltpu.VMEM((max(parts - 1, 1), block, width), BF16),
            pltpu.VMEM((slots, wide, rows), BF16),
            pltpu.VMEM((slots, wide, rows), BF16),
            dma((2, chunks)),
            dma((2, steps)),
            dma((2, slots)),
            dma((ticks, parts)),
            dma((ticks, parts)),
            dma((ticks, parts)),
            dma((parts,)),
            dma((ticks - 1, parts)),
            dma((ticks, parts)),
            dma((ticks, parts)),
            dma((ticks - 1, parts)),
        ],
        compiler_params=pltpu.CompilerParams(
            collective_id=0, has_side_effects=True, vmem_limit_bytes=67043328
        ),
    )(microbatch_slot, staleness, saved_inputs, up_weight, down_weight, upstream_grad, head_grad)
    return out


def solution(mesh):
    placed = (
        P("section", None, "tensor", None),
        P("section", None),
        P("section", None),
        P("section", None, "tensor"),
        P("section", "tensor", None),
        P("section", "tensor", None),
        P(None, "tensor", None),
    )
    return jax.shard_map(
        body,
        mesh=mesh,
        in_specs=placed,
        out_specs=P(None, "section", "tensor", None),
        check_vma=False,
    )
```

```python
import functools
import math

import jax
import jax.numpy as jnp
from jax import lax
from jax.experimental import pallas as pl
from jax.experimental.pallas import tpu as pltpu
from jax.sharding import PartitionSpec as P

MESH = pl.DeviceIdType.MESH
F32 = jnp.float32
BF16 = jnp.bfloat16
NT = (((1,), (1,)), ((), ()))


def learning_rates(total_rows, width, hidden_units):
    up_rate = 0.5 * math.sqrt(hidden_units) / (math.sqrt(total_rows) * width)
    down_rate = 0.5 / (math.sqrt(total_rows) * math.sqrt(hidden_units))
    return (up_rate, down_rate)


def dot(a, b):
    return jnp.dot(a, b, preferred_element_type=F32)


def dot_nt(a, b):
    return lax.dot_general(a, b, NT, preferred_element_type=F32)


def kernel(
    sections, parts, ticks, tile, groups, rates,
    slot_ref, stale_ref, saved_ref, up_hbm, down_hbm, first_ref, head_ref,
    out_ref, kept_hid, kept_hgr,
    up, down, hid, hgr, x_all, og, xs, ogs, acc, partial, landed, short, short_landed,
    old_hid, old_hgr,
    weight_sem, keep_sem, load_sem,
    x_send, x_recv, og_recv, first_send, head_send, sum_send, sum_recv, back_send,
):
    sec = lax.axis_index("section")
    me = lax.axis_index("tensor")
    is_last = sec == sections - 1
    not_first = sec > 0
    width, hidden = up.shape
    block = first_ref.shape[1]
    rows = block * parts
    chunks = hidden // tile
    zero_wide, renew_wide, last_wide, tick_wide = (tile * g for g in groups)

    def at(i, size=tile):
        if isinstance(i, int):
            return pl.ds(i * size, size)
        return pl.ds(pl.multiple_of(i * size, size), size)

    def peer(k):
        return lax.rem(me + k, parts)

    def weight_copies(i):
        return (
            pltpu.make_async_copy(up_hbm.at[0, :, at(i)], up.at[:, at(i)], weight_sem.at[0, i]),
            pltpu.make_async_copy(down_hbm.at[0, at(i), :], down.at[at(i), :], weight_sem.at[1, i]),
        )

    slots = old_hid.shape[0]

    def keep_copies(i):
        part = at(i, zero_wide)
        return (
            pltpu.make_async_copy(hid.at[part, :], kept_hid.at[part, :], keep_sem.at[0, i]),
            pltpu.make_async_copy(hgr.at[part, :], kept_hgr.at[part, :], keep_sem.at[1, i]),
        )

    def load_copies(i):
        s = i % slots
        part = at(i, last_wide)
        return (
            pltpu.make_async_copy(kept_hid.at[part, :], old_hid.at[s], load_sem.at[0, s]),
            pltpu.make_async_copy(kept_hgr.at[part, :], old_hgr.at[s], load_sem.at[1, s]),
        )

    def remote(src, dst, send, recv, s, p):
        return pltpu.make_async_remote_copy(
            src_ref=src, dst_ref=dst, send_sem=send, recv_sem=recv,
            device_id={"section": s, "tensor": p}, device_id_type=MESH,
        )

    def x_copies(t):
        return [
            remote(
                x_all.at[t, me], x_all.at[t, me],
                x_send.at[t, k - 1], x_recv.at[t, me], sec, peer(k),
            )
            for k in range(1, parts)
        ]

    def first_copies():
        return [
            remote(
                first_ref.at[0], og.at[0, me],
                first_send.at[k - 1], og_recv.at[0, me], sec, peer(k),
            )
            for k in range(1, parts)
        ]

    def head_copies(t):
        return [
            remote(
                head_ref.at[t], og.at[t + 1, me],
                head_send.at[t, k - 1], og_recv.at[t + 1, me], sec, peer(k),
            )
            for k in range(1, parts)
        ]

    def sum_copies(t):
        return [
            remote(
                partial.at[peer(k)] if t < ticks - 1 else short.at[peer(k)],
                landed.at[t, k - 1] if t < ticks - 1 else short_landed.at[k - 1],
                sum_send.at[t, k - 1], sum_recv.at[t, k - 1], sec, peer(k),
            )
            for k in range(1, parts)
        ]

    def back_copies(t):
        return [
            remote(
                out_ref.at[t, 0], og.at[t + 1, me],
                back_send.at[t, k], og_recv.at[t + 1, me], sec - 1, peer(k),
            )
            for k in range(parts)
        ]

    def arrived(ref, recv, t, first):
        for k in range(first, parts):
            here = ref.at[t, peer(k)]
            remote(here, here, recv.at[t, peer(k)], recv.at[t, peer(k)], sec, peer(1)).wait_recv()

    def start_weights(i, carry):
        for c in weight_copies(i):
            c.start()
        return carry

    lax.fori_loop(0, chunks, start_weights, 0)
    for t in range(ticks):
        x_all[t, me] = saved_ref[0, slot_ref[0, t]]
    og[0, me] = first_ref[0]

    @pl.when(is_last)
    def _():
        for t in range(ticks - 1):
            og[t + 1, me] = head_ref[t]

    barrier = pltpu.get_barrier_semaphore()
    for k in range(1, parts):
        pl.semaphore_signal(
            barrier, inc=1, device_id={"section": sec, "tensor": peer(k)}, device_id_type=MESH
        )

    @pl.when(jnp.logical_not(is_last))
    def _():
        for k in range(parts):
            pl.semaphore_signal(
                barrier, inc=1, device_id={"section": sec + 1, "tensor": peer(k)},
                device_id_type=MESH,
            )

    pl.semaphore_wait(barrier, jnp.where(not_first, 2 * parts - 1, parts - 1))

    for c in x_copies(0) + first_copies():
        c.start()

    arrived(x_all, x_recv, 0, 1)

    def x_of(t):
        return x_all[t].reshape(rows, width)

    def og_of(t):
        return og[t].reshape(rows, width)

    def flag(j, t):
        return jnp.where(j + stale_ref[0, j] <= t, 1.0, 0.0).astype(F32)

    def hidden_of(t, part):
        return jnp.maximum(dot(x_of(t), up[:, part]), 0.0).astype(BF16).T

    def grad_of(t, part, h):
        raw = dot_nt(down[part, :], og_of(t))
        return jnp.where(h.astype(F32) > 0, raw, 0.0).astype(BF16)

    def add_back(part):
        acc[...] += dot(up[:, part], hgr[part, :])

    def run(stage, depth, count):
        for i in range(depth):
            stage(i, range(0, i + 1))

        def inner(i, carry):
            stage(i, range(0, depth + 1))
            return carry

        lax.fori_loop(depth, count, inner, 0)
        for i in range(count, count + depth):
            stage(i, range(i - count + 1, depth + 1))

    def start_sum(t):
        total = acc[...].T.reshape(parts, block, width)
        partial[...] = total
        if t == ticks - 1:
            short[...] = total.astype(BF16)
        for c in sum_copies(t):
            c.start()

    def finish_sum(t):
        for c in sum_copies(t):
            c.wait_recv()
        total = partial[me]
        for k in range(1, parts):
            if t < ticks - 1:
                total = total + landed[t, k - 1]
            else:
                total = total + short_landed[k - 1].astype(F32)
        out_ref[t, 0] = total.astype(BF16)

    def between(t, i, count):
        @pl.when(i == min(count - 1, (3 * count + 7) // 8))
        def _():
            finish_sum(t)

            @pl.when(not_first)
            def _():
                for c in back_copies(t):
                    c.start()

    acc[...] = jnp.zeros_like(acc)

    def weights_here(i, wide):
        for k in range(wide // tile):
            for c in weight_copies(i * (wide // tile) + k):
                c.wait()

    def tick_zero(i, due):
        if 0 in due:
            weights_here(i, zero_wide)
        if 1 in due:
            for c in keep_copies(i - 1):
                c.start()
            add_back(at(i - 1, zero_wide))
        if 0 in due:
            part = at(i, zero_wide)
            h = hidden_of(0, part)
            hid[part, :] = h
            if isinstance(i, int):
                arrived(og, og_recv, 0, 1)
            hgr[part, :] = grad_of(0, part, h)
            if isinstance(i, int):
                later_copies()

    def later_copies():
        for t in range(1, ticks):
            for c in x_copies(t):
                c.start()

        @pl.when(is_last)
        def _():
            for t in range(ticks - 1):
                for c in head_copies(t):
                    c.start()

    run(tick_zero, 1, hidden // zero_wide)
    start_sum(0)
    for t in range(1, ticks):
        arrived(x_all, x_recv, t, 1)

    def turned(t):
        return x_of(t).astype(F32).T.astype(BF16)

    for t in range(1, ticks):
        last = t == ticks - 1
        if last:
            up_step, down_step = rates
            early, late = flag(t - 2, t).astype(BF16), flag(t - 1, t).astype(BF16)
            xs[:, :rows] = xs[:, :rows] * early
            xs[:, rows:] = turned(t - 1) * late
            ogs[:rows, :] = og_of(t - 2) * early
            ogs[rows:, :] = og_of(t - 1) * late
        else:
            xs[:, :rows] = turned(t - 1)
            up_step, down_step = rates[0] * flag(t - 1, t), rates[1] * flag(t - 1, t)

        wide = last_wide if last else renew_wide
        steps = hidden // wide

        def renew(i, due, t=t, last=last, wide=wide, steps=steps, up_step=up_step, down_step=down_step):
            between(t - 1, i, steps)
            part = at(i, wide)
            if last:
                for c in load_copies(i):
                    c.wait()
                weights_here(i, wide)
                s = i % slots
                g = jnp.concatenate([old_hgr[s], hgr[part, :]], axis=1)
                h = jnp.concatenate([old_hid[s], hid[part, :]], axis=1)
                x_side, og_side = xs[...], ogs[...]
            else:
                for k in range(wide // zero_wide):
                    for c in keep_copies(i * (wide // zero_wide) + k):
                        c.wait()
                g, h = hgr[part, :], hid[part, :]
                x_side, og_side = xs[:, :rows], og_of(t - 1)
            down[part, :] = (
                down[part, :].astype(F32) - down_step * dot(h, og_side)
            ).astype(BF16)
            up[:, part] = (
                up[:, part].astype(F32) - up_step * dot_nt(x_side, g)
            ).astype(BF16)
            hid[part, :] = hidden_of(t, part)
            if last:
                @pl.when(i + slots < steps)
                def _():
                    for c in load_copies(i + slots):
                        c.start()

        run(renew, 0, steps)

        @pl.when(is_last)
        def _():
            arrived(og, og_recv, t, 1)

        @pl.when(jnp.logical_not(is_last))
        def _():
            arrived(og, og_recv, t, 0)

        acc[...] = jnp.zeros_like(acc)
        for c in sum_copies(t - 1):
            c.wait_send()

        if not last:
            for k in range(min(slots, hidden // last_wide)):
                for c in load_copies(k):
                    c.start()

        def reload(i):
            for k in range(tick_wide // tile):
                for c in weight_copies(i * (tick_wide // tile) + k):
                    c.start()

        def tick(i, due, t=t, last=last):
            if not last:
                if isinstance(i, int):
                    if i >= 2:
                        reload(i - 2)
                else:
                    @pl.when(i >= 2)
                    def _():
                        reload(i - 2)
            if 1 in due:
                add_back(at(i - 1, tick_wide))
            if 0 in due:
                part = at(i, tick_wide)
                hgr[part, :] = grad_of(t, part, hid[part, :])

        run(tick, 1, hidden // tick_wide)
        if not last:
            reload(hidden // tick_wide - 1)
        start_sum(t)

    finish_sum(ticks - 1)

    for t in range(ticks):
        for c in x_copies(t):
            c.wait_send()
    for c in sum_copies(ticks - 1):
        c.wait_send()
    for c in first_copies():
        c.wait_send()
    for t in range(ticks - 1):
        @pl.when(is_last)
        def _():
            for c in head_copies(t):
                c.wait_send()

        @pl.when(not_first)
        def _():
            for c in back_copies(t):
                c.wait_send()


def body(
    saved_inputs, microbatch_slot, staleness, up_weight, down_weight, upstream_grad, head_grad
):
    block = saved_inputs.shape[2]
    ticks = microbatch_slot.shape[1]
    sections = lax.axis_size("section")
    parts = lax.axis_size("tensor")
    width, hidden = up_weight.shape[1:]
    rows = block * parts
    tile = min(512, hidden)
    chunks = hidden // tile
    groups = tuple(min(g, chunks) for g in (4, 8, 4, 8))
    kept, wide = hidden // (groups[0] * tile), groups[2] * tile
    slots = 2
    rates = learning_rates(rows, width, hidden * parts)
    vmem = pl.BlockSpec(memory_space=pltpu.VMEM)
    smem = pl.BlockSpec(memory_space=pltpu.SMEM)
    hbm = pl.BlockSpec(memory_space=pl.ANY)
    dma = pltpu.SemaphoreType.DMA
    out, _, _ = pl.pallas_call(
        functools.partial(kernel, sections, parts, ticks, tile, groups, rates),
        out_shape=(
            jax.ShapeDtypeStruct((ticks, 1, block, width), BF16),
            jax.ShapeDtypeStruct((hidden, rows), BF16),
            jax.ShapeDtypeStruct((hidden, rows), BF16),
        ),
        in_specs=[smem, smem, vmem, hbm, hbm, vmem, vmem],
        out_specs=(vmem, hbm, hbm),
        scratch_shapes=[
            pltpu.VMEM((width, hidden), BF16),
            pltpu.VMEM((hidden, width), BF16),
            pltpu.VMEM((hidden, rows), BF16),
            pltpu.VMEM((hidden, rows), BF16),
            pltpu.VMEM((ticks, parts, block, width), BF16),
            pltpu.VMEM((ticks, parts, block, width), BF16),
            pltpu.VMEM((width, 2 * rows), BF16),
            pltpu.VMEM((2 * rows, width), BF16),
            pltpu.VMEM((width, rows), F32),
            pltpu.VMEM((parts, block, width), F32),
            pltpu.VMEM((ticks - 1, max(parts - 1, 1), block, width), F32),
            pltpu.VMEM((parts, block, width), BF16),
            pltpu.VMEM((max(parts - 1, 1), block, width), BF16),
            pltpu.VMEM((slots, wide, rows), BF16),
            pltpu.VMEM((slots, wide, rows), BF16),
            dma((2, chunks)),
            dma((2, kept)),
            dma((2, slots)),
            dma((ticks, parts)),
            dma((ticks, parts)),
            dma((ticks, parts)),
            dma((parts,)),
            dma((ticks - 1, parts)),
            dma((ticks, parts)),
            dma((ticks, parts)),
            dma((ticks - 1, parts)),
        ],
        compiler_params=pltpu.CompilerParams(
            collective_id=0, has_side_effects=True, vmem_limit_bytes=67043328
        ),
    )(microbatch_slot, staleness, saved_inputs, up_weight, down_weight, upstream_grad, head_grad)
    return out


def solution(mesh):
    placed = (
        P("section", None, "tensor", None),
        P("section", None),
        P("section", None),
        P("section", None, "tensor"),
        P("section", "tensor", None),
        P("section", "tensor", None),
        P(None, "tensor", None),
    )
    return jax.shard_map(
        body,
        mesh=mesh,
        in_specs=placed,
        out_specs=P(None, "section", "tensor", None),
        check_vma=False,
    )
```

```python
import functools
import math

import jax
import jax.numpy as jnp
from jax import lax
from jax.experimental import pallas as pl
from jax.experimental.pallas import tpu as pltpu
from jax.sharding import PartitionSpec as P

MESH = pl.DeviceIdType.MESH
F32 = jnp.float32
BF16 = jnp.bfloat16
NT = (((1,), (1,)), ((), ()))


def learning_rates(total_rows, width, hidden_units):
    up_rate = 0.5 * math.sqrt(hidden_units) / (math.sqrt(total_rows) * width)
    down_rate = 0.5 / (math.sqrt(total_rows) * math.sqrt(hidden_units))
    return (up_rate, down_rate)


def dot(a, b):
    return jnp.dot(a, b, preferred_element_type=F32)


def dot_nt(a, b):
    return lax.dot_general(a, b, NT, preferred_element_type=F32)


def kernel(
    sections, parts, ticks, tile, groups, rates,
    slot_ref, stale_ref, saved_hbm, up_hbm, down_hbm, first_hbm, head_hbm,
    out_ref, kept_hid, kept_hgr,
    up, down, hid, hgr, x_all, og, xs, ogs, acc, partial, landed, short, short_landed,
    old_hid, old_hgr, saved,
    input_sem, weight_sem, keep_sem, load_sem,
    x_send, x_recv, og_recv, first_send, head_send, sum_send, sum_recv,
    half_send, half_recv, back_send,
):
    sec = lax.axis_index("section")
    me = lax.axis_index("tensor")
    is_last = sec == sections - 1
    not_first = sec > 0
    width, hidden = up.shape
    block = first_hbm.shape[1]
    rows = block * parts
    chunks = hidden // tile
    zero_wide, renew_wide, last_wide, tick_wide = (tile * g for g in groups)
    turn_late = block % 128 == 0
    half = width // 2

    def at(i, size=tile):
        if isinstance(i, int):
            return pl.ds(i * size, size)
        return pl.ds(pl.multiple_of(i * size, size), size)

    def peer(k):
        return lax.rem(me + k, parts)

    def weight_copies(i):
        return (
            pltpu.make_async_copy(up_hbm.at[0, :, at(i)], up.at[:, at(i)], weight_sem.at[0, i]),
            pltpu.make_async_copy(down_hbm.at[0, at(i), :], down.at[at(i), :], weight_sem.at[1, i]),
        )

    slots = old_hid.shape[0]

    def keep_copies(i):
        part = at(i, tick_wide)
        return (
            pltpu.make_async_copy(hid.at[part, :], kept_hid.at[part, :], keep_sem.at[0, i]),
            pltpu.make_async_copy(hgr.at[part, :], kept_hgr.at[part, :], keep_sem.at[1, i]),
        )

    def load_copies(i):
        s = i % slots
        part = at(i, last_wide)
        return (
            pltpu.make_async_copy(kept_hid.at[part, :], old_hid.at[s], load_sem.at[0, s]),
            pltpu.make_async_copy(kept_hgr.at[part, :], old_hgr.at[s], load_sem.at[1, s]),
        )

    def remote(src, dst, send, recv, s, p):
        return pltpu.make_async_remote_copy(
            src_ref=src, dst_ref=dst, send_sem=send, recv_sem=recv,
            device_id={"section": s, "tensor": p}, device_id_type=MESH,
        )

    def x_copies(t):
        return [
            remote(
                x_all.at[t, me], x_all.at[t, me],
                x_send.at[t, k - 1], x_recv.at[t, me], sec, peer(k),
            )
            for k in range(1, parts)
        ]

    def first_copies():
        return [
            remote(
                og.at[0, me], og.at[0, me],
                first_send.at[k - 1], og_recv.at[0, me], sec, peer(k),
            )
            for k in range(1, parts)
        ]

    def head_copies(t):
        return [
            remote(
                og.at[t + 1, me], og.at[t + 1, me],
                head_send.at[t, k - 1], og_recv.at[t + 1, me], sec, peer(k),
            )
            for k in range(1, parts)
        ]

    def sum_copies(t):
        return [
            remote(
                partial.at[peer(k)], landed.at[t, k - 1],
                sum_send.at[t, k - 1], sum_recv.at[t, k - 1], sec, peer(k),
            )
            for k in range(1, parts)
        ]

    def short_copies(n):
        return [
            remote(
                short.at[n, peer(k)], short_landed.at[n, k - 1],
                half_send.at[n, k - 1], half_recv.at[n, k - 1], sec, peer(k),
            )
            for k in range(1, parts)
        ]

    def back_copies(t):
        return [
            remote(
                out_ref.at[t, 0], og.at[t + 1, me],
                back_send.at[t, k], og_recv.at[t + 1, me], sec - 1, peer(k),
            )
            for k in range(parts)
        ]

    def arrived(ref, recv, t, first):
        for k in range(first, parts):
            here = ref.at[t, peer(k)]
            remote(here, here, recv.at[t, peer(k)], recv.at[t, peer(k)], sec, peer(1)).wait_recv()

    barrier = pltpu.get_barrier_semaphore()
    for k in range(1, parts):
        pl.semaphore_signal(
            barrier, inc=1, device_id={"section": sec, "tensor": peer(k)}, device_id_type=MESH
        )

    @pl.when(jnp.logical_not(is_last))
    def _():
        for k in range(parts):
            pl.semaphore_signal(
                barrier, inc=1, device_id={"section": sec + 1, "tensor": peer(k)},
                device_id_type=MESH,
            )

    saved_copy = pltpu.make_async_copy(saved_hbm.at[0], saved, input_sem.at[0])
    first_copy = pltpu.make_async_copy(first_hbm.at[0], og.at[0, me], input_sem.at[1])
    given = [
        pltpu.make_async_copy(head_hbm.at[t], og.at[t + 1, me], input_sem.at[2 + t])
        for t in range(ticks - 1)
    ]
    saved_copy.start()
    first_copy.start()

    def start_up(i, carry):
        weight_copies(i)[0].start()
        return carry

    lax.fori_loop(0, chunks, start_up, 0)

    @pl.when(is_last)
    def _():
        for c in given:
            c.start()

    saved_copy.wait()
    for t in range(ticks):
        x_all[t, me] = saved[slot_ref[0, t]]
    first_copy.wait()
    pl.semaphore_wait(barrier, jnp.where(not_first, 2 * parts - 1, parts - 1))

    for c in x_copies(0) + first_copies():
        c.start()

    arrived(x_all, x_recv, 0, 1)

    def x_of(t):
        return x_all[t].reshape(rows, width)

    def og_of(t):
        return og[t].reshape(rows, width)

    def flag(j, t):
        return jnp.where(j + stale_ref[0, j] <= t, 1.0, 0.0).astype(F32)

    def hidden_of(t, part):
        return jnp.maximum(dot(x_of(t), up[:, part]), 0.0).astype(BF16).T

    def grad_of(t, part, h):
        raw = dot_nt(down[part, :], og_of(t))
        return jnp.where(h.astype(F32) > 0, raw, 0.0).astype(BF16)

    def add_back(part):
        acc[...] += dot(up[:, part], hgr[part, :])

    def run(stage, depth, count):
        for i in range(depth):
            stage(i, range(0, i + 1))

        def inner(i, carry):
            stage(i, range(0, depth + 1))
            return carry

        lax.fori_loop(depth, count, inner, 0)
        for i in range(count, count + depth):
            stage(i, range(i - count + 1, depth + 1))

    def piece(p):
        return acc[:, p * block:(p + 1) * block]

    def start_sum(t):
        if turn_late:
            for p in range(parts):
                partial[p] = piece(p)
        else:
            partial[...] = acc[...].T.reshape(parts, block, width)
        for c in sum_copies(t):
            c.start()

    def finish_sum(t):
        for c in sum_copies(t):
            c.wait_recv()
        total = partial[me]
        for k in range(1, parts):
            total = total + landed[t, k - 1]
        out_ref[t, 0] = (total.T if turn_late else total).astype(BF16)

    def start_short(n):
        rows_of = pl.ds(n * half, half)
        if turn_late:
            for p in range(parts):
                total = acc[rows_of, p * block:(p + 1) * block]
                partial[p, rows_of, :] = total
                short[n, p] = total.astype(BF16)
        else:
            total = acc[rows_of, :].T.reshape(parts, block, half)
            partial[:, :, rows_of] = total
            short[n] = total.astype(BF16)
        for c in short_copies(n):
            c.start()

    def finish_short(n):
        cols = pl.ds(n * half, half)
        for c in short_copies(n):
            c.wait_recv()
        total = partial[me, cols, :] if turn_late else partial[me, :, cols]
        for k in range(1, parts):
            total = total + short_landed[n, k - 1].astype(F32)
        out_ref[ticks - 1, 0, :, cols] = (total.T if turn_late else total).astype(BF16)

    def between(t, i, count):
        @pl.when(i == min(count - 1, (3 * count + 7) // 8))
        def _():
            finish_sum(t)

            @pl.when(not_first)
            def _():
                for c in back_copies(t):
                    c.start()

    acc[...] = jnp.zeros_like(acc)

    def weights_here(i, wide, kinds=(0, 1)):
        for k in range(wide // tile):
            for kind in kinds:
                weight_copies(i * (wide // tile) + k)[kind].wait()

    def first_hidden(i, due):
        for k in range(zero_wide // tile):
            weight_copies(i * (zero_wide // tile) + k)[1].start()
        weights_here(i, zero_wide, (0,))
        part = at(i, zero_wide)
        hid[part, :] = hidden_of(0, part)

    run(first_hidden, 0, hidden // zero_wide)
    arrived(og, og_recv, 0, 1)
    for t in range(1, ticks):
        for c in x_copies(t):
            c.start()

    @pl.when(is_last)
    def _():
        for t in range(ticks - 1):
            given[t].wait()
            for c in head_copies(t):
                c.start()

    def tick_zero(i, due):
        if 0 in due:
            weights_here(i, tick_wide, (1,))
        if 1 in due:
            for c in keep_copies(i - 1):
                c.start()
            add_back(at(i - 1, tick_wide))
        if 0 in due:
            part = at(i, tick_wide)
            hgr[part, :] = grad_of(0, part, hid[part, :])

    run(tick_zero, 1, hidden // tick_wide)
    start_sum(0)
    for t in range(1, ticks):
        arrived(x_all, x_recv, t, 1)

    def turned(t):
        return x_of(t).astype(F32).T.astype(BF16)

    for t in range(1, ticks):
        last = t == ticks - 1
        if last:
            up_step, down_step = rates
            early, late = flag(t - 2, t).astype(BF16), flag(t - 1, t).astype(BF16)
            xs[:, :rows] = xs[:, :rows] * early
            xs[:, rows:] = turned(t - 1) * late
            ogs[:rows, :] = og_of(t - 2) * early
            ogs[rows:, :] = og_of(t - 1) * late
        else:
            xs[:, :rows] = turned(t - 1)
            up_step, down_step = rates[0] * flag(t - 1, t), rates[1] * flag(t - 1, t)

        wide = last_wide if last else renew_wide
        steps = hidden // wide

        def renew(i, due, t=t, last=last, wide=wide, steps=steps, up_step=up_step, down_step=down_step):
            between(t - 1, i, steps)
            part = at(i, wide)
            if last:
                for c in load_copies(i):
                    c.wait()
                weights_here(i, wide)
                s = i % slots
                g = jnp.concatenate([old_hgr[s], hgr[part, :]], axis=1)
                h = jnp.concatenate([old_hid[s], hid[part, :]], axis=1)
                x_side, og_side = xs[...], ogs[...]
            else:
                for k in range(wide // tick_wide):
                    for c in keep_copies(i * (wide // tick_wide) + k):
                        c.wait()
                g, h = hgr[part, :], hid[part, :]
                x_side, og_side = xs[:, :rows], og_of(t - 1)
            down[part, :] = (
                down[part, :].astype(F32) - down_step * dot(h, og_side)
            ).astype(BF16)
            up[:, part] = (
                up[:, part].astype(F32) - up_step * dot_nt(x_side, g)
            ).astype(BF16)
            hid[part, :] = hidden_of(t, part)
            if last:
                @pl.when(i + slots < steps)
                def _():
                    for c in load_copies(i + slots):
                        c.start()

        run(renew, 0, steps)

        @pl.when(is_last)
        def _():
            arrived(og, og_recv, t, 1)

        @pl.when(jnp.logical_not(is_last))
        def _():
            arrived(og, og_recv, t, 0)

        acc[...] = jnp.zeros_like(acc)
        for c in sum_copies(t - 1):
            c.wait_send()

        if not last:
            for k in range(min(slots, hidden // last_wide)):
                for c in load_copies(k):
                    c.start()

        def reload(i):
            for k in range(tick_wide // tile):
                for c in weight_copies(i * (tick_wide // tile) + k):
                    c.start()

        def tick(i, due, t=t, last=last):
            if not last:
                if isinstance(i, int):
                    if i >= 2:
                        reload(i - 2)
                else:
                    @pl.when(i >= 2)
                    def _():
                        reload(i - 2)
            if 1 in due:
                before = at(i - 1, tick_wide)
                if last:
                    acc[:half, :] += dot(up[:half, before], hgr[before, :])
                else:
                    add_back(before)
            if 0 in due:
                part = at(i, tick_wide)
                hgr[part, :] = grad_of(t, part, hid[part, :])

        run(tick, 1, hidden // tick_wide)
        if not last:
            reload(hidden // tick_wide - 1)
            start_sum(t)

    start_short(0)

    def other_half(i, due):
        part = at(i, zero_wide)
        acc[half:, :] += dot(up[half:, part], hgr[part, :])

    run(other_half, 0, hidden // zero_wide)
    start_short(1)
    finish_short(0)
    finish_short(1)

    for t in range(ticks):
        for c in x_copies(t):
            c.wait_send()
    for n in range(2):
        for c in short_copies(n):
            c.wait_send()
    for c in first_copies():
        c.wait_send()
    for t in range(ticks - 1):
        @pl.when(is_last)
        def _():
            for c in head_copies(t):
                c.wait_send()

        @pl.when(not_first)
        def _():
            for c in back_copies(t):
                c.wait_send()


def body(
    saved_inputs, microbatch_slot, staleness, up_weight, down_weight, upstream_grad, head_grad
):
    block = saved_inputs.shape[2]
    ticks = microbatch_slot.shape[1]
    sections = lax.axis_size("section")
    parts = lax.axis_size("tensor")
    width, hidden = up_weight.shape[1:]
    rows = block * parts
    tile = min(512, hidden)
    chunks = hidden // tile
    groups = tuple(min(g, chunks) for g in (16, 8, 4, 8))
    kept, wide = hidden // (groups[3] * tile), groups[2] * tile
    slots = 2
    if block % 128 == 0:
        lying, half_lying = (width, block), (width // 2, block)
    else:
        lying, half_lying = (block, width), (block, width // 2)
    rates = learning_rates(rows, width, hidden * parts)
    vmem = pl.BlockSpec(memory_space=pltpu.VMEM)
    smem = pl.BlockSpec(memory_space=pltpu.SMEM)
    hbm = pl.BlockSpec(memory_space=pl.ANY)
    dma = pltpu.SemaphoreType.DMA
    out, _, _ = pl.pallas_call(
        functools.partial(kernel, sections, parts, ticks, tile, groups, rates),
        out_shape=(
            jax.ShapeDtypeStruct((ticks, 1, block, width), BF16),
            jax.ShapeDtypeStruct((hidden, rows), BF16),
            jax.ShapeDtypeStruct((hidden, rows), BF16),
        ),
        in_specs=[smem, smem, hbm, hbm, hbm, hbm, hbm],
        out_specs=(vmem, hbm, hbm),
        scratch_shapes=[
            pltpu.VMEM((width, hidden), BF16),
            pltpu.VMEM((hidden, width), BF16),
            pltpu.VMEM((hidden, rows), BF16),
            pltpu.VMEM((hidden, rows), BF16),
            pltpu.VMEM((ticks, parts, block, width), BF16),
            pltpu.VMEM((ticks, parts, block, width), BF16),
            pltpu.VMEM((width, 2 * rows), BF16),
            pltpu.VMEM((2 * rows, width), BF16),
            pltpu.VMEM((width, rows), F32),
            pltpu.VMEM((parts, *lying), F32),
            pltpu.VMEM((ticks - 1, max(parts - 1, 1), *lying), F32),
            pltpu.VMEM((2, parts, *half_lying), BF16),
            pltpu.VMEM((2, max(parts - 1, 1), *half_lying), BF16),
            pltpu.VMEM((slots, wide, rows), BF16),
            pltpu.VMEM((slots, wide, rows), BF16),
            pltpu.VMEM(saved_inputs.shape[1:], BF16),
            dma((1 + ticks,)),
            dma((2, chunks)),
            dma((2, kept)),
            dma((2, slots)),
            dma((ticks, parts)),
            dma((ticks, parts)),
            dma((ticks, parts)),
            dma((parts,)),
            dma((ticks - 1, parts)),
            dma((ticks, parts)),
            dma((ticks, parts)),
            dma((2, parts)),
            dma((2, parts)),
            dma((ticks - 1, parts)),
        ],
        compiler_params=pltpu.CompilerParams(
            collective_id=0, has_side_effects=True, vmem_limit_bytes=67043328
        ),
    )(microbatch_slot, staleness, saved_inputs, up_weight, down_weight, upstream_grad, head_grad)
    return out


def solution(mesh):
    placed = (
        P("section", None, "tensor", None),
        P("section", None),
        P("section", None),
        P("section", None, "tensor"),
        P("section", "tensor", None),
        P("section", "tensor", None),
        P(None, "tensor", None),
    )
    return jax.shard_map(
        body,
        mesh=mesh,
        in_specs=placed,
        out_specs=P(None, "section", "tensor", None),
        check_vma=False,
    )
```

```python
import functools
import math

import jax
import jax.numpy as jnp
from jax import lax
from jax.experimental import pallas as pl
from jax.experimental.pallas import tpu as pltpu
from jax.sharding import PartitionSpec as P

MESH = pl.DeviceIdType.MESH
F32 = jnp.float32
BF16 = jnp.bfloat16
NT = (((1,), (1,)), ((), ()))


def learning_rates(total_rows, width, hidden_units):
    up_rate = 0.5 * math.sqrt(hidden_units) / (math.sqrt(total_rows) * width)
    down_rate = 0.5 / (math.sqrt(total_rows) * math.sqrt(hidden_units))
    return (up_rate, down_rate)


def dot(a, b):
    return jnp.dot(a, b, preferred_element_type=F32)


def dot_nt(a, b):
    return lax.dot_general(a, b, NT, preferred_element_type=F32)


def kernel(
    sections, parts, ticks, tile, groups, rates,
    slot_ref, stale_ref, saved_hbm, up_hbm, down_hbm, first_hbm, head_hbm,
    out_ref, kept_hid, kept_hgr,
    up, down, hid, hgr, x_all, og, xs, ogs, acc, partial, landed, short, short_landed,
    old_hid, old_hgr, saved,
    input_sem, weight_sem, keep_sem, load_sem,
    x_send, x_recv, og_recv, first_send, head_send, sum_send, sum_recv,
    half_send, half_recv, back_send,
):
    sec = lax.axis_index("section")
    me = lax.axis_index("tensor")
    is_last = sec == sections - 1
    not_first = sec > 0
    width, hidden = up.shape
    block = first_hbm.shape[1]
    rows = block * parts
    chunks = hidden // tile
    zero_wide, renew_wide, last_wide, tick_wide = (tile * g for g in groups)
    turn_late = block % 128 == 0
    half = width // 2

    def at(i, size=tile):
        if isinstance(i, int):
            return pl.ds(i * size, size)
        return pl.ds(pl.multiple_of(i * size, size), size)

    def peer(k):
        return lax.rem(me + k, parts)

    def weight_copies(i):
        return (
            pltpu.make_async_copy(up_hbm.at[0, :, at(i)], up.at[:, at(i)], weight_sem.at[0, i]),
            pltpu.make_async_copy(down_hbm.at[0, at(i), :], down.at[at(i), :], weight_sem.at[1, i]),
        )

    slots = old_hid.shape[0]

    def keep_copies(i):
        part = at(i, tick_wide)
        return (
            pltpu.make_async_copy(hid.at[part, :], kept_hid.at[part, :], keep_sem.at[0, i]),
            pltpu.make_async_copy(hgr.at[part, :], kept_hgr.at[part, :], keep_sem.at[1, i]),
        )

    def load_copies(i):
        s = i % slots
        part = at(i, last_wide)
        return (
            pltpu.make_async_copy(kept_hid.at[part, :], old_hid.at[s], load_sem.at[0, s]),
            pltpu.make_async_copy(kept_hgr.at[part, :], old_hgr.at[s], load_sem.at[1, s]),
        )

    def remote(src, dst, send, recv, s, p):
        return pltpu.make_async_remote_copy(
            src_ref=src, dst_ref=dst, send_sem=send, recv_sem=recv,
            device_id={"section": s, "tensor": p}, device_id_type=MESH,
        )

    def x_copies(t):
        return [
            remote(
                x_all.at[t, me], x_all.at[t, me],
                x_send.at[t, k - 1], x_recv.at[t, me], sec, peer(k),
            )
            for k in range(1, parts)
        ]

    def first_copies():
        return [
            remote(
                og.at[0, me], og.at[0, me],
                first_send.at[k - 1], og_recv.at[0, me], sec, peer(k),
            )
            for k in range(1, parts)
        ]

    def head_copies(t):
        return [
            remote(
                og.at[t + 1, me], og.at[t + 1, me],
                head_send.at[t, k - 1], og_recv.at[t + 1, me], sec, peer(k),
            )
            for k in range(1, parts)
        ]

    def sum_copies(t):
        return [
            remote(
                partial.at[peer(k)], landed.at[t, k - 1],
                sum_send.at[t, k - 1], sum_recv.at[t, k - 1], sec, peer(k),
            )
            for k in range(1, parts)
        ]

    def short_copies(n):
        return [
            remote(
                short.at[n, peer(k)], short_landed.at[n, k - 1],
                half_send.at[n, k - 1], half_recv.at[n, k - 1], sec, peer(k),
            )
            for k in range(1, parts)
        ]

    def back_copies(t):
        return [
            remote(
                out_ref.at[t, 0], og.at[t + 1, me],
                back_send.at[t, k], og_recv.at[t + 1, me], sec - 1, peer(k),
            )
            for k in range(parts)
        ]

    def arrived(ref, recv, t, first):
        for k in range(first, parts):
            here = ref.at[t, peer(k)]
            remote(here, here, recv.at[t, peer(k)], recv.at[t, peer(k)], sec, peer(1)).wait_recv()

    barrier = pltpu.get_barrier_semaphore()
    for k in range(1, parts):
        pl.semaphore_signal(
            barrier, inc=1, device_id={"section": sec, "tensor": peer(k)}, device_id_type=MESH
        )

    @pl.when(jnp.logical_not(is_last))
    def _():
        for k in range(parts):
            pl.semaphore_signal(
                barrier, inc=1, device_id={"section": sec + 1, "tensor": peer(k)},
                device_id_type=MESH,
            )

    saved_copy = pltpu.make_async_copy(saved_hbm.at[0], saved, input_sem.at[0])
    first_copy = pltpu.make_async_copy(first_hbm.at[0], og.at[0, me], input_sem.at[1])
    given = [
        pltpu.make_async_copy(head_hbm.at[t], og.at[t + 1, me], input_sem.at[2 + t])
        for t in range(ticks - 1)
    ]
    saved_copy.start()
    first_copy.start()

    def start_up(i, carry):
        weight_copies(i)[0].start()
        return carry

    lax.fori_loop(0, chunks, start_up, 0)

    @pl.when(is_last)
    def _():
        for c in given:
            c.start()

    saved_copy.wait()
    for t in range(ticks):
        x_all[t, me] = saved[slot_ref[0, t]]
    first_copy.wait()
    pl.semaphore_wait(barrier, jnp.where(not_first, 2 * parts - 1, parts - 1))

    for c in x_copies(0):
        c.start()
    arrived(x_all, x_recv, 0, 1)
    for c in first_copies():
        c.start()

    def x_of(t):
        return x_all[t].reshape(rows, width)

    def og_of(t):
        return og[t].reshape(rows, width)

    def flag(j, t):
        return jnp.where(j + stale_ref[0, j] <= t, 1.0, 0.0).astype(F32)

    def hidden_of(t, part):
        return jnp.maximum(dot(x_of(t), up[:, part]), 0.0).astype(BF16).T

    def grad_of(t, part, h):
        raw = dot_nt(down[part, :], og_of(t))
        return jnp.where(h.astype(F32) > 0, raw, 0.0).astype(BF16)

    def add_back(part):
        acc[...] += dot(up[:, part], hgr[part, :])

    def run(stage, depth, count):
        for i in range(depth):
            stage(i, range(0, i + 1))

        def inner(i, carry):
            stage(i, range(0, depth + 1))
            return carry

        lax.fori_loop(depth, count, inner, 0)
        for i in range(count, count + depth):
            stage(i, range(i - count + 1, depth + 1))

    def piece(p):
        return acc[:, p * block:(p + 1) * block]

    def start_sum(t):
        if turn_late:
            for p in range(parts):
                partial[p] = piece(p)
        else:
            partial[...] = acc[...].T.reshape(parts, block, width)
        for c in sum_copies(t):
            c.start()

    def finish_sum(t):
        for c in sum_copies(t):
            c.wait_recv()
        total = partial[me]
        for k in range(1, parts):
            total = total + landed[t, k - 1]
        out_ref[t, 0] = (total.T if turn_late else total).astype(BF16)

    def start_short(n):
        rows_of = pl.ds(n * half, half)
        if turn_late:
            for p in range(parts):
                total = acc[rows_of, p * block:(p + 1) * block]
                partial[p, rows_of, :] = total
                short[n, p] = total.astype(BF16)
        else:
            total = acc[rows_of, :].T.reshape(parts, block, half)
            partial[:, :, rows_of] = total
            short[n] = total.astype(BF16)
        for c in short_copies(n):
            c.start()

    def finish_short(n):
        cols = pl.ds(n * half, half)
        for c in short_copies(n):
            c.wait_recv()
        total = partial[me, cols, :] if turn_late else partial[me, :, cols]
        for k in range(1, parts):
            total = total + short_landed[n, k - 1].astype(F32)
        out_ref[ticks - 1, 0, :, cols] = (total.T if turn_late else total).astype(BF16)

    def between(t, i, count):
        @pl.when(i == min(count - 1, (3 * count + 7) // 8))
        def _():
            finish_sum(t)

            @pl.when(not_first)
            def _():
                for c in back_copies(t):
                    c.start()

    acc[...] = jnp.zeros_like(acc)

    def weights_here(i, wide, kinds=(0, 1)):
        for k in range(wide // tile):
            for kind in kinds:
                weight_copies(i * (wide // tile) + k)[kind].wait()

    def first_hidden(i, due):
        for k in range(zero_wide // tile):
            weight_copies(i * (zero_wide // tile) + k)[1].start()
        weights_here(i, zero_wide, (0,))
        part = at(i, zero_wide)
        hid[part, :] = hidden_of(0, part)

    run(first_hidden, 0, hidden // zero_wide)
    arrived(og, og_recv, 0, 1)
    for t in range(1, ticks):
        for c in x_copies(t):
            c.start()

    @pl.when(is_last)
    def _():
        for t in range(ticks - 1):
            given[t].wait()
            for c in head_copies(t):
                c.start()

    def tick_zero(i, due):
        if 0 in due:
            weights_here(i, tick_wide, (1,))
        if 1 in due:
            for c in keep_copies(i - 1):
                c.start()
            add_back(at(i - 1, tick_wide))
        if 0 in due:
            part = at(i, tick_wide)
            hgr[part, :] = grad_of(0, part, hid[part, :])

    run(tick_zero, 1, hidden // tick_wide)
    start_sum(0)
    for t in range(1, ticks):
        arrived(x_all, x_recv, t, 1)

    def turned(t):
        return x_of(t).astype(F32).T.astype(BF16)

    for t in range(1, ticks):
        last = t == ticks - 1
        if last:
            up_step, down_step = rates
            early, late = flag(t - 2, t).astype(BF16), flag(t - 1, t).astype(BF16)
            xs[:, :rows] = xs[:, :rows] * early
            xs[:, rows:] = turned(t - 1) * late
            ogs[:rows, :] = og_of(t - 2) * early
            ogs[rows:, :] = og_of(t - 1) * late
        else:
            xs[:, :rows] = turned(t - 1)
            up_step, down_step = rates[0] * flag(t - 1, t), rates[1] * flag(t - 1, t)

        wide = last_wide if last else renew_wide
        steps = hidden // wide

        def renew(i, due, t=t, last=last, wide=wide, steps=steps, up_step=up_step, down_step=down_step):
            between(t - 1, i, steps)
            part = at(i, wide)
            if last:
                for c in load_copies(i):
                    c.wait()
                weights_here(i, wide)
                s = i % slots
                g = jnp.concatenate([old_hgr[s], hgr[part, :]], axis=1)
                h = jnp.concatenate([old_hid[s], hid[part, :]], axis=1)
                x_side, og_side = xs[...], ogs[...]
            else:
                for k in range(wide // tick_wide):
                    for c in keep_copies(i * (wide // tick_wide) + k):
                        c.wait()
                g, h = hgr[part, :], hid[part, :]
                x_side, og_side = xs[:, :rows], og_of(t - 1)
            down[part, :] = (
                down[part, :].astype(F32) - down_step * dot(h, og_side)
            ).astype(BF16)
            up[:, part] = (
                up[:, part].astype(F32) - up_step * dot_nt(x_side, g)
            ).astype(BF16)
            hid[part, :] = hidden_of(t, part)
            if last:
                @pl.when(i + slots < steps)
                def _():
                    for c in load_copies(i + slots):
                        c.start()

        run(renew, 0, steps)

        @pl.when(is_last)
        def _():
            arrived(og, og_recv, t, 1)

        @pl.when(jnp.logical_not(is_last))
        def _():
            arrived(og, og_recv, t, 0)

        acc[...] = jnp.zeros_like(acc)
        for c in sum_copies(t - 1):
            c.wait_send()

        if not last:
            for k in range(min(slots, hidden // last_wide)):
                for c in load_copies(k):
                    c.start()

        def reload(i):
            for k in range(tick_wide // tile):
                for c in weight_copies(i * (tick_wide // tile) + k):
                    c.start()

        def tick(i, due, t=t, last=last):
            if not last:
                if isinstance(i, int):
                    if i >= 2:
                        reload(i - 2)
                else:
                    @pl.when(i >= 2)
                    def _():
                        reload(i - 2)
            if 1 in due:
                before = at(i - 1, tick_wide)
                if last:
                    acc[:half, :] += dot(up[:half, before], hgr[before, :])
                else:
                    add_back(before)
            if 0 in due:
                part = at(i, tick_wide)
                hgr[part, :] = grad_of(t, part, hid[part, :])

        run(tick, 1, hidden // tick_wide)
        if not last:
            reload(hidden // tick_wide - 1)
            start_sum(t)

    start_short(0)

    def other_half(i, due):
        part = at(i, zero_wide)
        acc[half:, :] += dot(up[half:, part], hgr[part, :])

    run(other_half, 0, hidden // zero_wide)
    start_short(1)
    finish_short(0)
    finish_short(1)

    for t in range(ticks):
        for c in x_copies(t):
            c.wait_send()
    for n in range(2):
        for c in short_copies(n):
            c.wait_send()
    for c in first_copies():
        c.wait_send()
    for t in range(ticks - 1):
        @pl.when(is_last)
        def _():
            for c in head_copies(t):
                c.wait_send()

        @pl.when(not_first)
        def _():
            for c in back_copies(t):
                c.wait_send()


def body(
    saved_inputs, microbatch_slot, staleness, up_weight, down_weight, upstream_grad, head_grad
):
    block = saved_inputs.shape[2]
    ticks = microbatch_slot.shape[1]
    sections = lax.axis_size("section")
    parts = lax.axis_size("tensor")
    width, hidden = up_weight.shape[1:]
    rows = block * parts
    tile = min(512, hidden)
    chunks = hidden // tile
    groups = tuple(min(g, chunks) for g in (16, 8, 4, 8))
    kept, wide = hidden // (groups[3] * tile), groups[2] * tile
    slots = 2
    if block % 128 == 0:
        lying, half_lying = (width, block), (width // 2, block)
    else:
        lying, half_lying = (block, width), (block, width // 2)
    rates = learning_rates(rows, width, hidden * parts)
    vmem = pl.BlockSpec(memory_space=pltpu.VMEM)
    smem = pl.BlockSpec(memory_space=pltpu.SMEM)
    hbm = pl.BlockSpec(memory_space=pl.ANY)
    dma = pltpu.SemaphoreType.DMA
    out, _, _ = pl.pallas_call(
        functools.partial(kernel, sections, parts, ticks, tile, groups, rates),
        out_shape=(
            jax.ShapeDtypeStruct((ticks, 1, block, width), BF16),
            jax.ShapeDtypeStruct((hidden, rows), BF16),
            jax.ShapeDtypeStruct((hidden, rows), BF16),
        ),
        in_specs=[smem, smem, hbm, hbm, hbm, hbm, hbm],
        out_specs=(vmem, hbm, hbm),
        scratch_shapes=[
            pltpu.VMEM((width, hidden), BF16),
            pltpu.VMEM((hidden, width), BF16),
            pltpu.VMEM((hidden, rows), BF16),
            pltpu.VMEM((hidden, rows), BF16),
            pltpu.VMEM((ticks, parts, block, width), BF16),
            pltpu.VMEM((ticks, parts, block, width), BF16),
            pltpu.VMEM((width, 2 * rows), BF16),
            pltpu.VMEM((2 * rows, width), BF16),
            pltpu.VMEM((width, rows), F32),
            pltpu.VMEM((parts, *lying), F32),
            pltpu.VMEM((ticks - 1, max(parts - 1, 1), *lying), F32),
            pltpu.VMEM((2, parts, *half_lying), BF16),
            pltpu.VMEM((2, max(parts - 1, 1), *half_lying), BF16),
            pltpu.VMEM((slots, wide, rows), BF16),
            pltpu.VMEM((slots, wide, rows), BF16),
            pltpu.VMEM(saved_inputs.shape[1:], BF16),
            dma((1 + ticks,)),
            dma((2, chunks)),
            dma((2, kept)),
            dma((2, slots)),
            dma((ticks, parts)),
            dma((ticks, parts)),
            dma((ticks, parts)),
            dma((parts,)),
            dma((ticks - 1, parts)),
            dma((ticks, parts)),
            dma((ticks, parts)),
            dma((2, parts)),
            dma((2, parts)),
            dma((ticks - 1, parts)),
        ],
        compiler_params=pltpu.CompilerParams(
            collective_id=0, has_side_effects=True, vmem_limit_bytes=67043328
        ),
    )(microbatch_slot, staleness, saved_inputs, up_weight, down_weight, upstream_grad, head_grad)
    return out


def solution(mesh):
    placed = (
        P("section", None, "tensor", None),
        P("section", None),
        P("section", None),
        P("section", None, "tensor"),
        P("section", "tensor", None),
        P("section", "tensor", None),
        P(None, "tensor", None),
    )
    return jax.shard_map(
        body,
        mesh=mesh,
        in_specs=placed,
        out_specs=P(None, "section", "tensor", None),
        check_vma=False,
    )
```

```python
import functools
import math

import jax
import jax.numpy as jnp
from jax import lax
from jax.experimental import pallas as pl
from jax.experimental.pallas import tpu as pltpu
from jax.sharding import PartitionSpec as P

MESH = pl.DeviceIdType.MESH
F32 = jnp.float32
BF16 = jnp.bfloat16
NT = (((1,), (1,)), ((), ()))


def learning_rates(total_rows, width, hidden_units):
    up_rate = 0.5 * math.sqrt(hidden_units) / (math.sqrt(total_rows) * width)
    down_rate = 0.5 / (math.sqrt(total_rows) * math.sqrt(hidden_units))
    return (up_rate, down_rate)


def dot(a, b):
    return jnp.dot(a, b, preferred_element_type=F32)


def dot_nt(a, b):
    return lax.dot_general(a, b, NT, preferred_element_type=F32)


def kernel(
    sections, parts, ticks, tile, groups, rates,
    slot_ref, stale_ref, saved_hbm, up_hbm, down_hbm, first_hbm, head_hbm,
    out_ref, kept_hid, kept_hgr,
    up, down, hid, hgr, x_all, og, xs, ogs, acc, partial, landed, short, short_landed,
    old_hid, old_hgr, saved,
    input_sem, weight_sem, keep_sem, load_sem,
    x_send, x_recv, og_recv, first_send, head_send, sum_send, sum_recv,
    half_send, half_recv, back_send,
):
    sec = lax.axis_index("section")
    me = lax.axis_index("tensor")
    is_last = sec == sections - 1
    not_first = sec > 0
    width, hidden = up.shape
    block = first_hbm.shape[1]
    rows = block * parts
    chunks = hidden // tile
    zero_wide, renew_wide, last_wide, tick_wide = (tile * g for g in groups)
    turn_late = block % 128 == 0
    half = width // 2

    def at(i, size=tile):
        if isinstance(i, int):
            return pl.ds(i * size, size)
        return pl.ds(pl.multiple_of(i * size, size), size)

    def peer(k):
        return lax.rem(me + k, parts)

    def weight_copies(i):
        return (
            pltpu.make_async_copy(up_hbm.at[0, :, at(i)], up.at[:, at(i)], weight_sem.at[0, i]),
            pltpu.make_async_copy(down_hbm.at[0, at(i), :], down.at[at(i), :], weight_sem.at[1, i]),
        )

    slots = old_hid.shape[0]

    def keep_copies(i):
        part = at(i, tick_wide)
        return (
            pltpu.make_async_copy(hid.at[part, :], kept_hid.at[part, :], keep_sem.at[0, i]),
            pltpu.make_async_copy(hgr.at[part, :], kept_hgr.at[part, :], keep_sem.at[1, i]),
        )

    def load_copies(i):
        s = i % slots
        part = at(i, last_wide)
        return (
            pltpu.make_async_copy(kept_hid.at[part, :], old_hid.at[s], load_sem.at[0, s]),
            pltpu.make_async_copy(kept_hgr.at[part, :], old_hgr.at[s], load_sem.at[1, s]),
        )

    def remote(src, dst, send, recv, s, p):
        return pltpu.make_async_remote_copy(
            src_ref=src, dst_ref=dst, send_sem=send, recv_sem=recv,
            device_id={"section": s, "tensor": p}, device_id_type=MESH,
        )

    def x_copies(t):
        return [
            remote(
                x_all.at[t, me], x_all.at[t, me],
                x_send.at[t, k - 1], x_recv.at[t, me], sec, peer(k),
            )
            for k in range(1, parts)
        ]

    def first_copies():
        return [
            remote(
                og.at[0, me], og.at[0, me],
                first_send.at[k - 1], og_recv.at[0, me], sec, peer(k),
            )
            for k in range(1, parts)
        ]

    def head_copies(t):
        return [
            remote(
                og.at[t + 1, me], og.at[t + 1, me],
                head_send.at[t, k - 1], og_recv.at[t + 1, me], sec, peer(k),
            )
            for k in range(1, parts)
        ]

    def sum_copies(t):
        return [
            remote(
                partial.at[peer(k)], landed.at[t, k - 1],
                sum_send.at[t, k - 1], sum_recv.at[t, k - 1], sec, peer(k),
            )
            for k in range(1, parts)
        ]

    def short_copies(n):
        return [
            remote(
                short.at[n, peer(k)], short_landed.at[n, k - 1],
                half_send.at[n, k - 1], half_recv.at[n, k - 1], sec, peer(k),
            )
            for k in range(1, parts)
        ]

    def back_copies(t):
        return [
            remote(
                out_ref.at[t, 0], og.at[t + 1, me],
                back_send.at[t, k], og_recv.at[t + 1, me], sec - 1, peer(k),
            )
            for k in range(parts)
        ]

    def arrived(ref, recv, t, first):
        for k in range(first, parts):
            here = ref.at[t, peer(k)]
            remote(here, here, recv.at[t, peer(k)], recv.at[t, peer(k)], sec, peer(1)).wait_recv()

    barrier = pltpu.get_barrier_semaphore()
    for k in range(1, parts):
        pl.semaphore_signal(
            barrier, inc=1, device_id={"section": sec, "tensor": peer(k)}, device_id_type=MESH
        )

    @pl.when(jnp.logical_not(is_last))
    def _():
        for k in range(parts):
            pl.semaphore_signal(
                barrier, inc=1, device_id={"section": sec + 1, "tensor": peer(k)},
                device_id_type=MESH,
            )

    saved_copy = pltpu.make_async_copy(saved_hbm.at[0], saved, input_sem.at[0])
    first_copy = pltpu.make_async_copy(first_hbm.at[0], og.at[0, me], input_sem.at[1])
    given = [
        pltpu.make_async_copy(head_hbm.at[t], og.at[t + 1, me], input_sem.at[2 + t])
        for t in range(ticks - 1)
    ]
    saved_copy.start()
    first_copy.start()

    def start_up(i, carry):
        weight_copies(i)[0].start()
        return carry

    lax.fori_loop(0, chunks, start_up, 0)

    @pl.when(is_last)
    def _():
        for c in given:
            c.start()

    saved_copy.wait()
    x_all[0, me] = saved[slot_ref[0, 0]]
    pl.semaphore_wait(barrier, jnp.where(not_first, 2 * parts - 1, parts - 1))

    for c in x_copies(0):
        c.start()
    for t in range(1, ticks):
        x_all[t, me] = saved[slot_ref[0, t]]
    first_copy.wait()
    arrived(x_all, x_recv, 0, 1)
    for c in first_copies():
        c.start()

    def x_of(t):
        return x_all[t].reshape(rows, width)

    def og_of(t):
        return og[t].reshape(rows, width)

    def flag(j, t):
        return jnp.where(j + stale_ref[0, j] <= t, 1.0, 0.0).astype(F32)

    def hidden_of(t, part):
        return jnp.maximum(dot(x_of(t), up[:, part]), 0.0).astype(BF16).T

    def grad_of(t, part, h):
        raw = dot_nt(down[part, :], og_of(t))
        return jnp.where(h.astype(F32) > 0, raw, 0.0).astype(BF16)

    def add_back(part):
        acc[...] += dot(up[:, part], hgr[part, :])

    def run(stage, depth, count):
        for i in range(depth):
            stage(i, range(0, i + 1))

        def inner(i, carry):
            stage(i, range(0, depth + 1))
            return carry

        lax.fori_loop(depth, count, inner, 0)
        for i in range(count, count + depth):
            stage(i, range(i - count + 1, depth + 1))

    def piece(p):
        return acc[:, p * block:(p + 1) * block]

    def start_sum(t):
        if turn_late:
            for p in range(parts):
                partial[p] = piece(p)
        else:
            partial[...] = acc[...].T.reshape(parts, block, width)
        for c in sum_copies(t):
            c.start()

    def finish_sum(t):
        for c in sum_copies(t):
            c.wait_recv()
        total = partial[me]
        for k in range(1, parts):
            total = total + landed[t, k - 1]
        out_ref[t, 0] = (total.T if turn_late else total).astype(BF16)

    def start_short(n):
        rows_of = pl.ds(n * half, half)
        if turn_late:
            for p in range(parts):
                total = acc[rows_of, p * block:(p + 1) * block]
                partial[p, rows_of, :] = total
                short[n, p] = total.astype(BF16)
        else:
            total = acc[rows_of, :].T.reshape(parts, block, half)
            partial[:, :, rows_of] = total
            short[n] = total.astype(BF16)
        for c in short_copies(n):
            c.start()

    def finish_short(n):
        cols = pl.ds(n * half, half)
        for c in short_copies(n):
            c.wait_recv()
        total = partial[me, cols, :] if turn_late else partial[me, :, cols]
        for k in range(1, parts):
            total = total + short_landed[n, k - 1].astype(F32)
        out_ref[ticks - 1, 0, :, cols] = (total.T if turn_late else total).astype(BF16)

    def between(t, i, count):
        @pl.when(i == min(count - 1, (3 * count + 7) // 8))
        def _():
            finish_sum(t)

            @pl.when(not_first)
            def _():
                for c in back_copies(t):
                    c.start()

    acc[...] = jnp.zeros_like(acc)

    def weights_here(i, wide, kinds=(0, 1)):
        for k in range(wide // tile):
            for kind in kinds:
                weight_copies(i * (wide // tile) + k)[kind].wait()

    def first_hidden(i, due):
        for k in range(zero_wide // tile):
            weight_copies(i * (zero_wide // tile) + k)[1].start()
        weights_here(i, zero_wide, (0,))
        part = at(i, zero_wide)
        hid[part, :] = hidden_of(0, part)

    run(first_hidden, 0, hidden // zero_wide)
    arrived(og, og_recv, 0, 1)
    for t in range(1, ticks):
        for c in x_copies(t):
            c.start()

    @pl.when(is_last)
    def _():
        for t in range(ticks - 1):
            given[t].wait()
            for c in head_copies(t):
                c.start()

    def tick_zero(i, due):
        if 0 in due:
            weights_here(i, tick_wide, (1,))
        if 1 in due:
            for c in keep_copies(i - 1):
                c.start()
            add_back(at(i - 1, tick_wide))
        if 0 in due:
            part = at(i, tick_wide)
            hgr[part, :] = grad_of(0, part, hid[part, :])

    run(tick_zero, 1, hidden // tick_wide)
    start_sum(0)
    for t in range(1, ticks):
        arrived(x_all, x_recv, t, 1)

    def turned(t):
        return x_of(t).astype(F32).T.astype(BF16)

    for t in range(1, ticks):
        last = t == ticks - 1
        if last:
            up_step, down_step = rates
            early, late = flag(t - 2, t).astype(BF16), flag(t - 1, t).astype(BF16)
            xs[:, :rows] = xs[:, :rows] * early
            xs[:, rows:] = turned(t - 1) * late
            ogs[:rows, :] = og_of(t - 2) * early
            ogs[rows:, :] = og_of(t - 1) * late
        else:
            xs[:, :rows] = turned(t - 1)
            up_step, down_step = rates[0] * flag(t - 1, t), rates[1] * flag(t - 1, t)

        wide = last_wide if last else renew_wide
        steps = hidden // wide

        def renew(i, due, t=t, last=last, wide=wide, steps=steps, up_step=up_step, down_step=down_step):
            between(t - 1, i, steps)
            part = at(i, wide)
            if last:
                for c in load_copies(i):
                    c.wait()
                weights_here(i, wide)
                s = i % slots
                g = jnp.concatenate([old_hgr[s], hgr[part, :]], axis=1)
                h = jnp.concatenate([old_hid[s], hid[part, :]], axis=1)
                x_side, og_side = xs[...], ogs[...]
            else:
                for k in range(wide // tick_wide):
                    for c in keep_copies(i * (wide // tick_wide) + k):
                        c.wait()
                g, h = hgr[part, :], hid[part, :]
                x_side, og_side = xs[:, :rows], og_of(t - 1)
            down[part, :] = (
                down[part, :].astype(F32) - down_step * dot(h, og_side)
            ).astype(BF16)
            up[:, part] = (
                up[:, part].astype(F32) - up_step * dot_nt(x_side, g)
            ).astype(BF16)
            hid[part, :] = hidden_of(t, part)
            if last:
                @pl.when(i + slots < steps)
                def _():
                    for c in load_copies(i + slots):
                        c.start()

        run(renew, 0, steps)

        @pl.when(is_last)
        def _():
            arrived(og, og_recv, t, 1)

        @pl.when(jnp.logical_not(is_last))
        def _():
            arrived(og, og_recv, t, 0)

        acc[...] = jnp.zeros_like(acc)
        for c in sum_copies(t - 1):
            c.wait_send()

        if not last:
            for k in range(min(slots, hidden // last_wide)):
                for c in load_copies(k):
                    c.start()

        def reload(i):
            for k in range(tick_wide // tile):
                for c in weight_copies(i * (tick_wide // tile) + k):
                    c.start()

        def tick(i, due, t=t, last=last):
            if not last:
                if isinstance(i, int):
                    if i >= 2:
                        reload(i - 2)
                else:
                    @pl.when(i >= 2)
                    def _():
                        reload(i - 2)
            if 1 in due:
                before = at(i - 1, tick_wide)
                if last:
                    acc[:half, :] += dot(up[:half, before], hgr[before, :])
                else:
                    add_back(before)
            if 0 in due:
                part = at(i, tick_wide)
                hgr[part, :] = grad_of(t, part, hid[part, :])

        run(tick, 1, hidden // tick_wide)
        if not last:
            reload(hidden // tick_wide - 1)
            start_sum(t)

    start_short(0)

    def other_half(i, due):
        part = at(i, zero_wide)
        acc[half:, :] += dot(up[half:, part], hgr[part, :])

    run(other_half, 0, hidden // zero_wide)
    start_short(1)
    finish_short(0)
    finish_short(1)

    for t in range(ticks):
        for c in x_copies(t):
            c.wait_send()
    for n in range(2):
        for c in short_copies(n):
            c.wait_send()
    for c in first_copies():
        c.wait_send()
    for t in range(ticks - 1):
        @pl.when(is_last)
        def _():
            for c in head_copies(t):
                c.wait_send()

        @pl.when(not_first)
        def _():
            for c in back_copies(t):
                c.wait_send()


def body(
    saved_inputs, microbatch_slot, staleness, up_weight, down_weight, upstream_grad, head_grad
):
    block = saved_inputs.shape[2]
    ticks = microbatch_slot.shape[1]
    sections = lax.axis_size("section")
    parts = lax.axis_size("tensor")
    width, hidden = up_weight.shape[1:]
    rows = block * parts
    tile = min(512, hidden)
    chunks = hidden // tile
    groups = tuple(min(g, chunks) for g in (16, 8, 4, 8))
    kept, wide = hidden // (groups[3] * tile), groups[2] * tile
    slots = 2
    if block % 128 == 0:
        lying, half_lying = (width, block), (width // 2, block)
    else:
        lying, half_lying = (block, width), (block, width // 2)
    rates = learning_rates(rows, width, hidden * parts)
    vmem = pl.BlockSpec(memory_space=pltpu.VMEM)
    smem = pl.BlockSpec(memory_space=pltpu.SMEM)
    hbm = pl.BlockSpec(memory_space=pl.ANY)
    dma = pltpu.SemaphoreType.DMA
    out, _, _ = pl.pallas_call(
        functools.partial(kernel, sections, parts, ticks, tile, groups, rates),
        out_shape=(
            jax.ShapeDtypeStruct((ticks, 1, block, width), BF16),
            jax.ShapeDtypeStruct((hidden, rows), BF16),
            jax.ShapeDtypeStruct((hidden, rows), BF16),
        ),
        in_specs=[smem, smem, hbm, hbm, hbm, hbm, hbm],
        out_specs=(vmem, hbm, hbm),
        scratch_shapes=[
            pltpu.VMEM((width, hidden), BF16),
            pltpu.VMEM((hidden, width), BF16),
            pltpu.VMEM((hidden, rows), BF16),
            pltpu.VMEM((hidden, rows), BF16),
            pltpu.VMEM((ticks, parts, block, width), BF16),
            pltpu.VMEM((ticks, parts, block, width), BF16),
            pltpu.VMEM((width, 2 * rows), BF16),
            pltpu.VMEM((2 * rows, width), BF16),
            pltpu.VMEM((width, rows), F32),
            pltpu.VMEM((parts, *lying), F32),
            pltpu.VMEM((ticks - 1, max(parts - 1, 1), *lying), F32),
            pltpu.VMEM((2, parts, *half_lying), BF16),
            pltpu.VMEM((2, max(parts - 1, 1), *half_lying), BF16),
            pltpu.VMEM((slots, wide, rows), BF16),
            pltpu.VMEM((slots, wide, rows), BF16),
            pltpu.VMEM(saved_inputs.shape[1:], BF16),
            dma((1 + ticks,)),
            dma((2, chunks)),
            dma((2, kept)),
            dma((2, slots)),
            dma((ticks, parts)),
            dma((ticks, parts)),
            dma((ticks, parts)),
            dma((parts,)),
            dma((ticks - 1, parts)),
            dma((ticks, parts)),
            dma((ticks, parts)),
            dma((2, parts)),
            dma((2, parts)),
            dma((ticks - 1, parts)),
        ],
        compiler_params=pltpu.CompilerParams(
            collective_id=0, has_side_effects=True, vmem_limit_bytes=67043328
        ),
    )(microbatch_slot, staleness, saved_inputs, up_weight, down_weight, upstream_grad, head_grad)
    return out


def solution(mesh):
    placed = (
        P("section", None, "tensor", None),
        P("section", None),
        P("section", None),
        P("section", None, "tensor"),
        P("section", "tensor", None),
        P("section", "tensor", None),
        P(None, "tensor", None),
    )
    return jax.shard_map(
        body,
        mesh=mesh,
        in_specs=placed,
        out_specs=P(None, "section", "tensor", None),
        check_vma=False,
    )
```
